32 devices in a mesh: det: 8 (over z, x), vis: 4 (over y, core).
Axes of the slice: x: 2, y: 2, z: 4, core: 2. Of those that a mesh axis runs over, the one named last changes fastest.
Arguments:
- template: bfloat16 [4096, 1070], P(('det', 'vis')), may hold values from -16 to 16
- science: bfloat16 [8, 4, 256, 1024], P('det', 'vis'), may hold values from -24 to 24
- good_pixels: int32 [8, 4, 256, 1024], P('det', 'vis'), may hold values 0 or 1
- dither: int32 [8, 4, 2], P('det', 'vis'), may hold values from -8 to 8
- routes: int32 [8, 4, 256, 1], P('det', 'vis'), may hold values from 0 to 7; in each aligned block of 256 rows (0 to 255, 256 to 511, ..., all dimensions but the last counted through in order) at most 64 rows name the same one
Outputs:
- patch_rows: bfloat16 [8, 4, 512, 1024], P('det', 'vis')
The draws below stay inside these ranges and needn't reach their ends.
Inputs may be any that keep to these rules, and one draw needn't show every extreme that they name: `routes`: in each device's 256 rows no owner is named by more than 64 rows.
All inputs are finite; a program needn't handle non-finite values. No bound on the sum of `good_pixels` on one device may be relied on, other than what follows from the above.
Results may differ from the reference program's by a relative error of at most 0.00055.
The reference program's roundings to bfloat16 on the way count: a program that leaves them out, or rounds other values in their place, can miss the bound.
Values may be sent and summed in bfloat16 or wider, within the bound.
No kernel may reach another device: no remote copies, remote signals or barrier semaphores. Data moves between devices by JAX's collectives and lax.ppermute only.
A program may use at most 64 MiB of HBM per device.

```python
import math
import jax
import jax.numpy as jnp
import numpy as np
from jax import lax

W = 1024
R = 256
TAPS = 31
NB = 3
DMAX = 8
HALF = 15
HW = 23
WT = 1070
SH = 128
CAP = 64
N_DET = 8
N_VIS = 4


def sky_field(key):
    region_rows = N_DET * N_VIS * SH
    rows_index = (jnp.arange(region_rows, dtype=jnp.int32) // (2 * R)).astype(jnp.float32)
    spread = float(max(N_DET - 1, 1))
    ramp_factor = 1.0 + 2.0 * rows_index / spread
    raw_values = jnp.clip(jax.random.normal(jax.random.fold_in(key, 11), (region_rows, WT), jnp.float32), -5.0, 5.0)
    return raw_values * ramp_factor[:, None]


def pointing(key):
    return jax.random.randint(jax.random.fold_in(key, 13), (N_DET, N_VIS, 2), -DMAX, DMAX + 1, dtype=jnp.int32)


def draw_template(key, part):
    noise_field = jnp.clip(jax.random.normal(jax.random.fold_in(key, 12), (N_DET * N_VIS * SH, WT), jnp.float32), -5.0, 5.0)
    return jnp.clip(sky_field(key) + 0.05 * noise_field, -16.0, 16.0).astype(jnp.bfloat16)


def draw_dither(key, part):
    return pointing(key)


def draw_science(key, part):
    padded = jnp.pad(sky_field(key), ((DMAX + 1, DMAX + 1), (1, 1)))
    shifts = pointing(key)
    row_base = jnp.arange(N_DET, dtype=jnp.int32)[:, None] * (2 * R) + jnp.arange(N_VIS, dtype=jnp.int32)[None, :] // 2 * R + shifts[:, :, 0] + DMAX + 1
    col_base = HW + shifts[:, :, 1] + 1
    row_index = row_base[:, :, None, None] + jnp.arange(R, dtype=jnp.int32)[None, None, :, None]
    col_index = col_base[:, :, None, None] + jnp.arange(W, dtype=jnp.int32)[None, None, None, :]
    center = padded[row_index, col_index]
    beside_all = padded[row_index - 1, col_index] + padded[row_index + 1, col_index]
    beside_all = beside_all + padded[row_index, col_index - 1] + padded[row_index, col_index + 1]
    level = 0.4 * (1.0 + jnp.arange(N_DET, dtype=jnp.float32) / float(max(N_DET - 1, 1)))
    noise_field = jnp.clip(jax.random.normal(jax.random.fold_in(key, 14), (N_DET, N_VIS, R, W), jnp.float32), -5.0, 5.0)
    values = 1.4 * (0.4 * center + 0.15 * beside_all) + level[:, None, None, None] * noise_field
    return jnp.clip(values, -24.0, 24.0).astype(jnp.bfloat16)


def place_ends(values, own_key, low, top_value):
    longest = values.shape.index(max(values.shape))
    spots = []
    for shift in (0, 1):
        where = [jax.random.randint(jax.random.fold_in(own_key, axis), (), 0, length) for axis, length in enumerate(values.shape)]
        where[longest] = (where[longest] + shift) % values.shape[longest]
        spots.append(tuple(where))
    return values.at[spots[0]].set(low).at[spots[1]].set(top_value)


def shared_out(rng, own, number, rows, count, top, most, skew):
    order = jax.random.permutation(rng, count)
    heavy_load, ordinary = shares(count, rows * top, most, skew, True), shares(count, rows * top, most, skew, False)
    places = jnp.arange(count)

    def named(tallies, rotation):
        used = int((tallies > 0).sum())
        fixed = max(1, used // 4)
        shifted = fixed + (places - fixed + rotation * (used - fixed)) % max(1, count - fixed)
        return jnp.zeros((count,), jnp.int32).at[order[jnp.where(places < fixed, places, shifted)]].set(jnp.asarray(tallies, jnp.int32))

    tallies = jnp.where(number % 4 == 0, named(heavy_load, number // 4), named(ordinary, number - number // 4 - 1))
    mixed = jax.random.permutation(jax.random.fold_in(own, 3), count)
    giver, sink = mixed[0:count // 2 * 2:2], mixed[1:count // 2 * 2:2]
    slack = jnp.minimum(tallies[giver] - 1, most - tallies[sink]) // 2
    slack = jnp.where((giver == order[0]) | (sink == order[0]) | (tallies[sink] == 0), 0, jnp.maximum(slack, 0))
    shifted = jax.random.randint(jax.random.fold_in(own, 4), (count // 2,), 0, 1 << 20) % (slack + 1)
    tallies = tallies.at[giver].add(-shifted).at[sink].add(shifted)
    labels = jnp.searchsorted(jnp.cumsum(tallies), jnp.arange(rows * top), side="right").astype(jnp.int32)
    grid = labels.reshape(top, rows).T
    grid = grid[jax.random.permutation(jax.random.fold_in(own, 1), rows)]
    rotation = jax.random.randint(jax.random.fold_in(own, 2), (rows, 1), 0, top)
    return jnp.take_along_axis(grid, (jnp.arange(top)[None, :] + rotation) % top, axis=1)


def shares(amount, total, limit, skew, full):
    loads = [(1 << 20) // math.isqrt(grade ** skew) + 1 for grade in range(1, amount + 1)]
    largest = limit if full else min(limit, max(-(-total // amount), total * loads[0] // sum(loads)))
    least = 1 if total - largest >= amount - 1 else 0
    holding, spare = [largest] + [least] * (amount - 1), total - largest - least * (amount - 1)
    while spare > 0:
        free = [i for i in range(1, amount) if holding[i] < largest] or [i for i in range(1, amount) if holding[i] < limit]
        mass, budget = sum([loads[i] for i in free]), spare
        for i in free:
            extra = min(limit - holding[i], max(1, budget * loads[i] // mass), spare)
            holding[i] = holding[i] + extra
            spare = spare - extra
    return np.array(holding)


def setup_inputs(seed: int = 0) -> dict:
    key_list = jax.random.split(jax.random.key(seed), 6)
    template = draw_template(jax.random.fold_in(key_list[5], 71), 0)
    science = draw_science(jax.random.fold_in(key_list[5], 71), 0)
    good_pixels = place_ends((jax.random.randint(key_list[2], (N_DET, N_VIS, R, W), 0, 16) < 15).astype(jnp.int32), jax.random.fold_in(key_list[2], 1), 0, 1)
    dither = draw_dither(jax.random.fold_in(key_list[5], 71), 0)
    routes_keys = jax.random.split(jax.random.fold_in(key_list[4], 1), N_DET * N_VIS * R // R)
    routes_turns = jax.random.permutation(jax.random.fold_in(key_list[4], 3), N_DET * N_VIS * R // R)
    routes = jax.vmap(lambda own, number: shared_out(jax.random.fold_in(key_list[4], 2), own, number, R, N_DET, 1, CAP, 1))(routes_keys, routes_turns).reshape((N_DET, N_VIS, R, 1))
    return {"template": template, "science": science, "good_pixels": good_pixels, "dither": dither, "routes": routes}


widths_list = (0.7, 1.5, 3.0)
epsilon = 1e-06

def tap_table():
    offsets = jnp.arange(TAPS, dtype=jnp.float32) - HALF
    widths = jnp.array(widths_list, dtype=jnp.float32)
    curves = jnp.exp(-(offsets[None, :] * offsets[None, :]) / (2.0 * widths[:, None] * widths[:, None]))
    curves = curves / lax.optimization_barrier(jnp.sum(curves, axis=1, keepdims=True))
    return curves.astype(jnp.bfloat16)

def solve_small(matrix, vector):
    lower_part = jnp.linalg.cholesky(matrix)
    dimension = matrix.shape[0]
    forward = []
    for row_at in range(dimension):
        running = vector[row_at]
        for col_at in range(row_at):
            running = running - lower_part[row_at, col_at] * forward[col_at]
        forward.append(running / lower_part[row_at, row_at])
    backward = [None] * dimension
    for row_at in range(dimension - 1, -1, -1):
        running = forward[row_at]
        for col_at in range(row_at + 1, dimension):
            running = running - lower_part[col_at, row_at] * backward[col_at]
        backward[row_at] = running / lower_part[row_at, row_at]
    return jnp.stack(backward)

def basis_images(tile_pixels, curves):
    across = curves[:, None, None, :]
    smeared = lax.conv_general_dilated(tile_pixels[None, None], across, (1, 1), 'VALID', preferred_element_type=jnp.float32)
    smeared = smeared.astype(jnp.bfloat16)
    downward = curves[:, None, :, None]
    basis_set = lax.conv_general_dilated(smeared, downward, (1, 1), 'VALID', feature_group_count=NB, preferred_element_type=jnp.float32)
    return basis_set[0]

def local_stats(basis_set, signal, weight):
    flattened = basis_set.reshape(NB, -1)
    design = jnp.concatenate([flattened, jnp.ones((1, flattened.shape[1]), dtype=jnp.float32)], axis=0)
    weighted = design * weight.reshape(1, -1)
    signal_flat = signal.reshape(-1)
    gram_sums = jnp.einsum('kp,lp->kl', weighted, design, precision=lax.Precision.HIGHEST)
    moment = jnp.einsum('kp,p->k', weighted, signal_flat, precision=lax.Precision.HIGHEST)
    power_sum = jnp.sum(weighted[NB] * signal_flat * signal_flat)
    return (gram_sums, moment, power_sum)

def place_rows(values, targets, owners, capacity):
    row_count = values.shape[0]
    chosen_owner = (targets[:, None] == jnp.arange(owners, dtype=jnp.int32)[None, :]).astype(jnp.int32)
    rank_within = lax.optimization_barrier(jnp.sum((jnp.cumsum(chosen_owner, axis=0) - chosen_owner) * chosen_owner, axis=1)).astype(jnp.int32)
    slot_index = targets * capacity + rank_within
    matches = jnp.arange(owners * capacity, dtype=jnp.int32)[:, None] == slot_index[None, :]
    sources = lax.optimization_barrier(jnp.sum(jnp.where(matches, jnp.arange(row_count, dtype=jnp.int32)[None, :], 0), axis=1)).astype(jnp.int32)
    filled = jnp.any(matches, axis=1)
    return jnp.where(filled[:, None], jnp.take(values, sources, axis=0), jnp.zeros((), values.dtype))

def reference(template, science, good_pixels, dither, routes):
    curves = tap_table()
    padded = jnp.pad(template, ((HW, HW), (0, 0)))
    device_ids = jnp.arange(N_DET * N_VIS, dtype=jnp.int32)

    def tile_basis(device):
        det_at = device // N_VIS
        vis_at = device % N_VIS
        shifts = dither[det_at, vis_at]
        start_row = (det_at * (2 * R) + vis_at // 2 * R + shifts[0] - HALF + HW).astype(jnp.int32)
        start_col = (HW + shifts[1] - HALF).astype(jnp.int32)
        tile_pixels = lax.dynamic_slice(padded, (start_row, start_col), (R + 2 * HALF, W + 2 * HALF))
        return (basis_images(tile_pixels, curves), det_at, vis_at)

    def first_pass(device):
        basis_set, det_at, vis_at = tile_basis(device)
        signal = science[det_at, vis_at].astype(jnp.float32)
        weight = good_pixels[det_at, vis_at].astype(jnp.float32)
        gram_sums, moment, power_sum = local_stats(basis_set, signal, weight)
        return jnp.concatenate([gram_sums.reshape(-1), moment, power_sum[None]])
    statistics = lax.map(first_pass, device_ids)
    totals = lax.optimization_barrier(jnp.sum(statistics.reshape(N_DET, 2, 2, -1), axis=(0, 1)))
    gram_all = totals[:, :(NB + 1) * (NB + 1)].reshape(2, NB + 1, NB + 1)
    moment_all = totals[:, (NB + 1) * (NB + 1):(NB + 1) * (NB + 2)]
    power_all = totals[:, (NB + 1) * (NB + 2)]
    identity = jnp.eye(NB + 1, dtype=jnp.float32)
    coeffs = jnp.stack([solve_small(gram_all[visit_at] + identity, moment_all[visit_at]) for visit_at in range(2)])
    quadratic = jnp.einsum('pk,pkl,pl->p', coeffs, gram_all, coeffs, precision=lax.Precision.HIGHEST)
    residual = power_all - 2.0 * lax.optimization_barrier(jnp.sum(coeffs * moment_all, axis=1)) + quadratic
    scales = 1.0 / jnp.sqrt(residual / (gram_all[:, NB, NB] + 1.0) + epsilon)

    def second_pass(device):
        basis_set, det_at, vis_at = tile_basis(device)
        visit_at = vis_at % 2
        signal = science[det_at, vis_at].astype(jnp.float32)
        weight = good_pixels[det_at, vis_at].astype(jnp.float32)
        chosen = coeffs[visit_at]
        model_image = jnp.einsum('b,brw->rw', chosen[:NB], basis_set, precision=lax.Precision.HIGHEST) + chosen[NB]
        difference = weight * (signal - model_image)
        significance = (difference * scales[visit_at]).astype(jnp.bfloat16)
        return place_rows(significance, routes[det_at, vis_at, :, 0], N_DET, CAP)
    buffers = lax.map(second_pass, device_ids)
    buffers = buffers.reshape(N_DET, N_VIS, N_DET, CAP, W)
    return jnp.transpose(buffers, (2, 1, 0, 3, 4)).reshape(N_DET, N_VIS, N_DET * CAP, W)
```

```python
import jax
import jax.numpy as jnp
import numpy as np
from jax import lax
from jax.experimental import pallas as pl
from jax.experimental.pallas import tpu as pltpu
from jax.sharding import PartitionSpec as P

TAPS = 31
NB = 3
HALF = 15
HW = 23
DMAX = HW - HALF
EDGE = 32
LANES = 128
ROWS = 128
STATS = 16
DIRECT = 16

widths_list = (0.7, 1.5, 3.0)
epsilon = 1e-06


def tap_table():
    offsets = np.arange(TAPS, dtype=np.float32) - np.float32(HALF)
    widths = np.array(widths_list, dtype=np.float32)
    curves = np.exp(
        -(offsets[None, :] * offsets[None, :])
        / (np.float32(2.0) * widths[:, None] * widths[:, None])
    )
    curves = curves / np.sum(curves, axis=1, keepdims=True, dtype=np.float32)
    return curves.astype(jnp.dtype(jnp.bfloat16))


def band_at(curves, tap):
    inside = (tap >= 0) & (tap < TAPS)
    return np.where(inside, curves[:, np.clip(tap, 0, TAPS - 1)], 0).astype(curves.dtype)


def band_tables():
    curves = tap_table()
    span = 2 * DMAX
    inputs = np.arange(2 * LANES + span)[:, None]
    across = band_at(curves, inputs - np.arange(LANES)[None, :] - span)
    across = np.transpose(across, (1, 0, 2)).reshape(2 * LANES + span, NB * LANES)
    outputs = np.arange(ROWS + span)[:, None]
    first = EDGE - HALF - DMAX
    downward = band_at(curves, np.arange(ROWS + 2 * EDGE)[None, :] - outputs - first)
    return jnp.asarray(across), jnp.asarray(downward)


def fit_kernel(parity, own, other, own_edge, other_edge, across, downward, science, good, basis, stats, area, smeared):
    share = own.shape[0]
    used = own.shape[1]
    width = science.shape[1]
    height = science.shape[0]
    area[:, width:] = jnp.zeros((area.shape[0], area.shape[1] - width), area.dtype)

    def arrange(low_edge, low, high, high_edge):
        area[0:EDGE, 0:used] = low_edge[...]
        area[EDGE : EDGE + share, 0:used] = low[...]
        area[EDGE + share : EDGE + 2 * share, 0:used] = high[...]
        area[EDGE + 2 * share :, 0:used] = high_edge[...]

    @pl.when(parity[0] == 0)
    def _():
        arrange(own_edge, own, other, other_edge)

    @pl.when(parity[0] == 1)
    def _():
        arrange(other_edge, other, own, own_edge)

    for at in range(0, width, LANES):
        block = jnp.dot(
            area[:, at : at + 2 * LANES], across[...], preferred_element_type=jnp.float32
        ).astype(jnp.bfloat16)
        for b in range(NB):
            smeared[b, :, at : at + LANES] = block[:, b * LANES : (b + 1) * LANES]
    for at in range(0, height, ROWS):
        for b in range(NB):
            basis[b, at : at + ROWS, :] = jnp.dot(
                downward[b], smeared[b, at : at + ROWS + 2 * EDGE, :],
                preferred_element_type=jnp.float32,
            )

    group = 16

    def step(index, sums):
        rows = pl.ds(pl.multiple_of(index * group, group), group)
        sums = list(sums)
        for at in range(0, width, LANES):
            cols = slice(at, at + LANES)
            weight = good[rows, cols].astype(jnp.float32)
            signal = science[rows, cols].astype(jnp.float32)
            terms = [weight * basis[b, rows, cols] for b in range(NB)]
            lit = weight * signal
            values = [terms[k] * terms[l] for k in range(NB) for l in range(k, NB)]
            values += terms + [weight]
            values += [terms[k] * signal for k in range(NB)] + [lit, lit * signal]
            sums = [total + value for total, value in zip(sums, values)]
        return tuple(sums)

    zero = jnp.zeros((group, LANES), jnp.float32)
    sums = lax.fori_loop(0, height // group, step, (zero,) * 15)
    for k, total in enumerate(sums):
        stats[k : k + 1, :] = jnp.sum(total, axis=0, keepdims=True)
    stats[15:16, :] = jnp.zeros((1, LANES), jnp.float32)


def place_kernel(targets, place, *, owners, capacity):
    rows = targets.shape[1]
    wanted = targets[...]
    chosen = lax.broadcasted_iota(jnp.int32, (owners, rows), 0) == wanted
    earlier = lax.broadcasted_iota(jnp.int32, (rows, rows), 0) < lax.broadcasted_iota(
        jnp.int32, (rows, rows), 1
    )
    before = jnp.dot(
        chosen.astype(jnp.float32).astype(jnp.bfloat16),
        earlier.astype(jnp.float32).astype(jnp.bfloat16),
        preferred_element_type=jnp.float32,
    )
    rank = jnp.sum(jnp.where(chosen, before, 0.0), axis=0, keepdims=True).astype(jnp.int32)
    slot = wanted * capacity + rank
    matches = lax.broadcasted_iota(jnp.int32, place.shape, 0) == slot
    place[...] = matches.astype(jnp.float32).astype(jnp.bfloat16)


def solve_small(gram, vector):
    size = NB + 1
    matrix = [[gram[r][c] + (1.0 if r == c else 0.0) for c in range(size)] for r in range(size)]
    lower = [[None] * size for _ in range(size)]
    for c in range(size):
        running = matrix[c][c]
        for k in range(c):
            running = running - lower[c][k] * lower[c][k]
        lower[c][c] = jnp.sqrt(running)
        for r in range(c + 1, size):
            running = matrix[r][c]
            for k in range(c):
                running = running - lower[r][k] * lower[c][k]
            lower[r][c] = running / lower[c][c]
    forward = []
    for r in range(size):
        running = vector[r]
        for c in range(r):
            running = running - lower[r][c] * forward[c]
        forward.append(running / lower[r][r])
    backward = [None] * size
    for r in range(size - 1, -1, -1):
        running = forward[r]
        for c in range(r + 1, size):
            running = running - lower[c][r] * backward[c]
        backward[r] = running / lower[r][r]
    return backward


def send_kernel(stats, basis, science, good, place, *refs):
    outs, significance = refs[:-1], refs[-1]
    totals = jnp.sum(stats[...], axis=1, keepdims=True)
    value = [totals[k : k + 1, :] for k in range(15)]
    gram = [[None] * (NB + 1) for _ in range(NB + 1)]
    at = 0
    for k in range(NB):
        for l in range(k, NB):
            gram[k][l] = gram[l][k] = value[at]
            at += 1
    for k in range(NB + 1):
        gram[k][NB] = gram[NB][k] = value[at]
        at += 1
    moment = value[at : at + NB + 1]
    power = value[at + NB + 1]
    coeffs = solve_small(gram, moment)
    cross = sum(coeffs[k] * moment[k] for k in range(NB + 1))
    quadratic = sum(
        coeffs[k] * gram[k][l] * coeffs[l] for k in range(NB + 1) for l in range(NB + 1)
    )
    residual = power - 2.0 * cross + quadratic
    scale = 1.0 / jnp.sqrt(residual / (gram[NB][NB] + 1.0) + epsilon)

    width = science.shape[1]
    group = 16
    spread = lambda x: jnp.broadcast_to(x, (group, LANES))
    weights = [spread(c) for c in coeffs]
    scale = spread(scale)

    def step(index, carry):
        rows = pl.ds(pl.multiple_of(index * group, group), group)
        for start in range(0, width, LANES):
            cols = slice(start, start + LANES)
            model = weights[0] * basis[0, rows, cols]
            for b in range(1, NB):
                model = model + weights[b] * basis[b, rows, cols]
            model = model + weights[NB]
            difference = good[rows, cols].astype(jnp.float32) * (
                science[rows, cols].astype(jnp.float32) - model
            )
            significance[rows, cols] = (difference * scale).astype(jnp.bfloat16)
        return carry

    lax.fori_loop(0, science.shape[0] // group, step, 0)
    length = outs[0].shape[0]
    for k, out in enumerate(outs):
        out[...] = jnp.dot(
            place[k * length : (k + 1) * length, :], significance[...],
            preferred_element_type=jnp.float32,
        ).astype(jnp.bfloat16)


def whole(memory=pltpu.VMEM):
    return pl.BlockSpec(memory_space=memory)


def body(template, science, good_pixels, dither, routes):
    det_count = lax.axis_size("det")
    vis_count = lax.axis_size("vis")
    count = det_count * vis_count
    vis_at = lax.axis_index("vis")
    det_at = lax.axis_index("det")
    parity = vis_at % 2
    share = template.shape[0]
    height, width = science.shape[2:]
    both = ("det", "vis")

    outgoing = lax.dynamic_slice_in_dim(template, parity * (share - EDGE), EDGE, axis=0)
    seam = [(i, i + 1) for i in range(1, count - 1, 2)]
    own_edge = lax.ppermute(outgoing, both, seam + [(j, i) for i, j in seam])
    pairs = [(i, i ^ 1) for i in range(vis_count)]
    other = lax.ppermute(template, "vis", pairs)
    other_edge = lax.ppermute(own_edge, "vis", pairs)

    across, downward = band_tables()
    shifts = dither[0, 0]
    across = lax.dynamic_slice_in_dim(across, DMAX - shifts[1], 2 * LANES, axis=0)
    downward = lax.dynamic_slice_in_dim(downward, DMAX + shifts[0], ROWS, axis=1)

    owners = det_count
    capacity = max(2, 2 * height // owners)
    slots = owners * capacity
    direct = owners <= DIRECT
    targets = routes.reshape(1, height)
    if direct:
        targets = (targets - det_at) % owners
    place = pl.pallas_call(
        lambda *refs: place_kernel(*refs, owners=owners, capacity=capacity),
        out_shape=jax.ShapeDtypeStruct((slots, height), jnp.bfloat16),
        in_specs=[whole()],
        out_specs=whole(),
        name="place_rows",
    )(targets)

    science = science[0, 0]
    good = good_pixels[0, 0]
    basis, stats = pl.pallas_call(
        fit_kernel,
        out_shape=(
            jax.ShapeDtypeStruct((NB, height, width), jnp.float32),
            jax.ShapeDtypeStruct((STATS, LANES), jnp.float32),
        ),
        in_specs=[whole(pltpu.SMEM)] + [whole()] * 8,
        out_specs=(whole(), whole()),
        scratch_shapes=[
            pltpu.VMEM((2 * share + 2 * EDGE, width + LANES), jnp.bfloat16),
            pltpu.VMEM((NB, 2 * share + 2 * EDGE, width), jnp.bfloat16),
        ],
        name="fit_basis",
    )(parity.reshape(1), template, other, own_edge, other_edge, across, downward, science, good)

    for axis, size, first in (("det", det_count, 1), ("vis", vis_count, 2)):
        stride = first
        while stride < size:
            stats = stats + lax.ppermute(stats, axis, [(i, i ^ stride) for i in range(size)])
            stride *= 2

    parts = owners if direct else 1
    length = slots // parts
    blocks = pl.pallas_call(
        send_kernel,
        out_shape=[jax.ShapeDtypeStruct((length, width), jnp.bfloat16)] * parts,
        in_specs=[whole()] * 5,
        out_specs=[whole()] * parts,
        scratch_shapes=[pltpu.VMEM((height, width), jnp.bfloat16)],
        name="send_rows",
    )(stats, basis, science, good, place)

    if not direct:
        result = lax.all_to_all(blocks[0], "det", split_axis=0, concat_axis=0, tiled=True)
        return result[None, None]
    result = jnp.zeros((slots, width), jnp.bfloat16)
    result = lax.dynamic_update_slice_in_dim(result, blocks[0], det_at * length, axis=0)
    for d in range(1, owners):
        block = lax.ppermute(blocks[d], "det", [(i, (i + d) % owners) for i in range(owners)])
        result = lax.dynamic_update_slice_in_dim(
            result, block, (det_at - d) % owners * length, axis=0
        )
    return result[None, None]


def solution(mesh):
    placed = (
        P(("det", "vis"), None),
        P("det", "vis", None, None),
        P("det", "vis", None, None),
        P("det", "vis", None),
        P("det", "vis", None, None),
    )
    return jax.shard_map(
        body, mesh=mesh, in_specs=placed, out_specs=P("det", "vis", None, None), check_vma=False
    )
```

```python
import jax
import jax.numpy as jnp
import numpy as np
from jax import lax
from jax.experimental import pallas as pl
from jax.experimental.pallas import tpu as pltpu
from jax.sharding import PartitionSpec as P

TAPS = 31
NB = 3
HALF = 15
HW = 23
DMAX = HW - HALF
EDGE = 32
LANES = 128
ROWS = 128
STATS = 16
DIRECT = 16
GUARD = 8
GRANT = 16 << 20

widths_list = (0.7, 1.5, 3.0)
epsilon = 1e-06


def tap_table():
    offsets = np.arange(TAPS, dtype=np.float32) - np.float32(HALF)
    widths = np.array(widths_list, dtype=np.float32)
    curves = np.exp(
        -(offsets[None, :] * offsets[None, :])
        / (np.float32(2.0) * widths[:, None] * widths[:, None])
    )
    curves = curves / np.sum(curves, axis=1, keepdims=True, dtype=np.float32)
    return curves.astype(jnp.dtype(jnp.bfloat16))


def band_at(curves, tap):
    inside = (tap >= 0) & (tap < TAPS)
    return np.where(inside, curves[:, np.clip(tap, 0, TAPS - 1)], 0).astype(curves.dtype)


def band_tables():
    curves = tap_table()
    span = 2 * DMAX
    inputs = np.arange(-GUARD, 2 * LANES + span)[:, None]
    across = band_at(curves, inputs - np.arange(LANES)[None, :] - span)
    across = np.transpose(across, (1, 0, 2)).reshape(-1, NB * LANES)
    outputs = np.arange(-GUARD, ROWS + span)[:, None]
    first = EDGE - HALF - DMAX
    downward = band_at(curves, np.arange(ROWS + 2 * EDGE)[None, :] - outputs - first)
    return jnp.asarray(across.astype(np.float32)), jnp.asarray(downward.astype(np.float32))


def fit_kernel(own, other, own_edge, other_edge, across, downward, science, good, basis, stats, area, smeared):
    share = own.shape[0]
    used = own.shape[1]
    width = science.shape[1]
    height = science.shape[0]
    area[:, width:] = jnp.zeros((area.shape[0], area.shape[1] - width), area.dtype)

    def arrange(low_edge, low, high, high_edge):
        area[0:EDGE, 0:used] = low_edge[...]
        area[EDGE : EDGE + share, 0:used] = low[...]
        area[EDGE + share : EDGE + 2 * share, 0:used] = high[...]
        area[EDGE + 2 * share :, 0:used] = high_edge[...]

    parity = lax.axis_index("vis") % 2

    @pl.when(parity == 0)
    def _():
        arrange(own_edge, own, other, other_edge)

    @pl.when(parity == 1)
    def _():
        arrange(other_edge, other, own, own_edge)

    for at in range(0, width, LANES):
        block = jnp.dot(
            area[:, at : at + 2 * LANES], across[...], preferred_element_type=jnp.float32
        ).astype(jnp.bfloat16)
        for b in range(NB):
            smeared[b, :, at : at + LANES] = block[:, b * LANES : (b + 1) * LANES]
    for at in range(0, height, ROWS):
        for b in range(NB):
            basis[b, at : at + ROWS, :] = jnp.dot(
                downward[b], smeared[b, at : at + ROWS + 2 * EDGE, :],
                preferred_element_type=jnp.float32,
            )

    group = 16

    def step(index, sums):
        rows = pl.ds(pl.multiple_of(index * group, group), group)
        sums = list(sums)
        for at in range(0, width, LANES):
            cols = slice(at, at + LANES)
            weight = good[rows, cols].astype(jnp.float32)
            signal = science[rows, cols].astype(jnp.float32)
            terms = [weight * basis[b, rows, cols] for b in range(NB)]
            lit = weight * signal
            values = [terms[k] * terms[l] for k in range(NB) for l in range(k, NB)]
            values += terms + [weight]
            values += [terms[k] * signal for k in range(NB)] + [lit, lit * signal]
            sums = [total + value for total, value in zip(sums, values)]
        return tuple(sums)

    zero = jnp.zeros((group, LANES), jnp.float32)
    sums = lax.fori_loop(0, height // group, step, (zero,) * 15)
    for k, total in enumerate(sums):
        stats[k : k + 1, :] = jnp.sum(total, axis=0, keepdims=True)
    stats[15:16, :] = jnp.zeros((1, LANES), jnp.float32)


def edge_kernel(template, edge, sem):
    start = lax.axis_index("vis") % 2 * (template.shape[0] - EDGE)
    rows = pl.ds(pl.multiple_of(start, EDGE), EDGE)
    copy = pltpu.make_async_copy(template.at[rows, :], edge, sem)
    copy.start()
    copy.wait()


def collect_kernel(*refs, shifts):
    blocks, result, sem = refs[: len(shifts)], refs[-2], refs[-1]
    at = lax.axis_index("det")
    owners = lax.axis_size("det")
    length = blocks[0].shape[0]
    copies = []
    for k, shift in enumerate(shifts):
        start = pl.multiple_of((at - shift + owners) % owners * length, length)
        copies.append(
            pltpu.make_async_copy(blocks[k], result.at[pl.ds(start, length), :], sem.at[k])
        )
    for copy in copies:
        copy.start()
    for copy in copies:
        copy.wait()


def prepare_kernel(
    dither, routes, across, downward, template, science, good,
    band, column, place, own, signal, weight, far_across, far_downward, shifts, targets, sem,
    *, owners, capacity, direct
):
    moves = (
        (routes, targets), (dither, shifts), (across, far_across), (downward, far_downward),
        (template, own), (science, signal), (good, weight),
    )
    copies = [pltpu.make_async_copy(*move, sem.at[k]) for k, move in enumerate(moves)]
    for copy in copies:
        copy.start()
    copies[0].wait()
    rows = targets.shape[1]
    wanted = targets[...]
    if direct:
        wanted = wanted - lax.axis_index("det")
        wanted = jnp.where(wanted < 0, wanted + owners, wanted)
    chosen = lax.broadcasted_iota(jnp.int32, (owners, rows), 0) == wanted
    earlier = lax.broadcasted_iota(jnp.int32, (rows, rows), 0) < lax.broadcasted_iota(
        jnp.int32, (rows, rows), 1
    )
    before = jnp.dot(
        chosen.astype(jnp.float32).astype(jnp.bfloat16),
        earlier.astype(jnp.float32).astype(jnp.bfloat16),
        preferred_element_type=jnp.float32,
    )
    rank = jnp.sum(jnp.where(chosen, before, 0.0), axis=0, keepdims=True).astype(jnp.int32)
    slot = wanted * capacity + rank
    matches = lax.broadcasted_iota(jnp.int32, place.shape, 0) == slot
    place[...] = matches.astype(jnp.float32).astype(jnp.bfloat16)
    for copy in copies[1:4]:
        copy.wait()
    size = far_across.shape[0]
    turned = pltpu.roll(far_across[...], size - GUARD - DMAX + shifts[1], 0)
    band[...] = turned[: band.shape[0]].astype(band.dtype)
    size = far_downward.shape[1]
    for b in range(NB):
        turned = pltpu.roll(far_downward[b], size - GUARD - DMAX - shifts[0], 0)
        column[b] = turned[:ROWS].astype(column.dtype)
    for copy in copies[4:]:
        copy.wait()


def solve_small(gram, vector):
    size = NB + 1
    matrix = [[gram[r][c] + (1.0 if r == c else 0.0) for c in range(size)] for r in range(size)]
    lower = [[None] * size for _ in range(size)]
    for c in range(size):
        running = matrix[c][c]
        for k in range(c):
            running = running - lower[c][k] * lower[c][k]
        lower[c][c] = jnp.sqrt(running)
        for r in range(c + 1, size):
            running = matrix[r][c]
            for k in range(c):
                running = running - lower[r][k] * lower[c][k]
            lower[r][c] = running / lower[c][c]
    forward = []
    for r in range(size):
        running = vector[r]
        for c in range(r):
            running = running - lower[r][c] * forward[c]
        forward.append(running / lower[r][r])
    backward = [None] * size
    for r in range(size - 1, -1, -1):
        running = forward[r]
        for c in range(r + 1, size):
            running = running - lower[c][r] * backward[c]
        backward[r] = running / lower[r][r]
    return backward


def send_kernel(stats, arrived, basis, science, good, place, *refs):
    outs, significance = refs[:-1], refs[-1]
    totals = jnp.sum(stats[...] + arrived[...], axis=1, keepdims=True)
    value = [totals[k : k + 1, :] for k in range(15)]
    gram = [[None] * (NB + 1) for _ in range(NB + 1)]
    at = 0
    for k in range(NB):
        for l in range(k, NB):
            gram[k][l] = gram[l][k] = value[at]
            at += 1
    for k in range(NB + 1):
        gram[k][NB] = gram[NB][k] = value[at]
        at += 1
    moment = value[at : at + NB + 1]
    power = value[at + NB + 1]
    coeffs = solve_small(gram, moment)
    cross = sum(coeffs[k] * moment[k] for k in range(NB + 1))
    quadratic = sum(
        coeffs[k] * gram[k][l] * coeffs[l] for k in range(NB + 1) for l in range(NB + 1)
    )
    residual = power - 2.0 * cross + quadratic
    scale = 1.0 / jnp.sqrt(residual / (gram[NB][NB] + 1.0) + epsilon)

    width = science.shape[1]
    group = 16
    spread = lambda x: jnp.broadcast_to(x, (group, LANES))
    weights = [spread(c) for c in coeffs]
    scale = spread(scale)

    def step(index, carry):
        rows = pl.ds(pl.multiple_of(index * group, group), group)
        for start in range(0, width, LANES):
            cols = slice(start, start + LANES)
            model = weights[0] * basis[0, rows, cols]
            for b in range(1, NB):
                model = model + weights[b] * basis[b, rows, cols]
            model = model + weights[NB]
            difference = good[rows, cols].astype(jnp.float32) * (
                science[rows, cols].astype(jnp.float32) - model
            )
            significance[rows, cols] = (difference * scale).astype(jnp.bfloat16)
        return carry

    lax.fori_loop(0, science.shape[0] // group, step, 0)
    length = outs[0].shape[0]
    for k, out in enumerate(outs):
        out[...] = jnp.dot(
            place[k * length : (k + 1) * length, :], significance[...],
            preferred_element_type=jnp.float32,
        ).astype(jnp.bfloat16)


def whole(memory=pltpu.VMEM):
    return pl.BlockSpec(memory_space=memory)


def near(*arrays):
    return [pltpu.with_memory_space_constraint(array, pltpu.VMEM) for array in arrays]


def far(*arrays):
    return [pltpu.with_memory_space_constraint(array, pltpu.HBM) for array in arrays]


def body(template, science, good_pixels, dither, routes):
    det_count = lax.axis_size("det")
    vis_count = lax.axis_size("vis")
    count = det_count * vis_count
    share = template.shape[0]
    height, width = science.shape[2:]
    both = ("det", "vis")

    outgoing = pl.pallas_call(
        edge_kernel,
        out_shape=pltpu.VMEM((EDGE, template.shape[1]), template.dtype),
        in_specs=[whole(pltpu.HBM)],
        out_specs=whole(),
        scratch_shapes=[pltpu.SemaphoreType.DMA],
        compiler_params=pltpu.CompilerParams(vmem_limit_bytes=GRANT),
        name="edge",
    )(*far(template))
    seam = [(i, i + 1) for i in range(1, count - 1, 2)]
    own_edge = lax.ppermute(outgoing, both, seam + [(j, i) for i, j in seam])
    pairs = [(i, i ^ 1) for i in range(vis_count)]
    other = lax.ppermute(template, "vis", pairs)

    owners = det_count
    capacity = max(2, 2 * height // owners)
    slots = owners * capacity
    direct = owners <= DIRECT
    targets = routes.reshape(1, height)
    tables = band_tables()
    band, column, place, own, science, good = pl.pallas_call(
        lambda *refs: prepare_kernel(*refs, owners=owners, capacity=capacity, direct=direct),
        out_shape=(
            pltpu.VMEM((2 * LANES, NB * LANES), jnp.bfloat16),
            pltpu.VMEM((NB, ROWS, ROWS + 2 * EDGE), jnp.bfloat16),
            pltpu.VMEM((slots, height), jnp.bfloat16),
            pltpu.VMEM(template.shape, template.dtype),
            pltpu.VMEM((height, width), science.dtype),
            pltpu.VMEM((height, width), good_pixels.dtype),
        ),
        in_specs=[whole(pltpu.HBM)] * 7,
        out_specs=(whole(),) * 6,
        scratch_shapes=[pltpu.VMEM(table.shape, table.dtype) for table in tables]
        + [pltpu.SMEM((2,), jnp.int32), pltpu.VMEM((1, height), jnp.int32)]
        + [pltpu.SemaphoreType.DMA((7,))],
        compiler_params=pltpu.CompilerParams(vmem_limit_bytes=GRANT),
        name="prepare",
    )(*far(dither.reshape(2), targets, *tables, template, science[0, 0], good_pixels[0, 0]))
    own_edge, column = lax.optimization_barrier((own_edge, column))
    other_edge = lax.ppermute(own_edge, "vis", pairs)

    basis, stats = pl.pallas_call(
        fit_kernel,
        out_shape=(
            pltpu.VMEM((NB, height, width), jnp.float32),
            pltpu.VMEM((STATS, LANES), jnp.float32),
        ),
        in_specs=[whole()] * 8,
        out_specs=(whole(), whole()),
        scratch_shapes=[
            pltpu.VMEM((2 * share + 2 * EDGE, width + LANES), jnp.bfloat16),
            pltpu.VMEM((NB, 2 * share + 2 * EDGE, width), jnp.bfloat16),
        ],
        compiler_params=pltpu.CompilerParams(vmem_limit_bytes=GRANT),
        name="fit_basis",
    )(*near(own, other, own_edge, other_edge, band, column, science, good))

    arrived = jnp.zeros_like(stats)
    for axis, size, first in (("det", det_count, 1), ("vis", vis_count, 2)):
        stride = first
        while stride < size:
            stats = stats + arrived
            arrived = lax.ppermute(stats, axis, [(i, i ^ stride) for i in range(size)])
            stride *= 2

    parts = owners if direct else 1
    length = slots // parts
    blocks = pl.pallas_call(
        send_kernel,
        out_shape=[pltpu.VMEM((length, width), jnp.bfloat16)] * parts,
        in_specs=[whole()] * 6,
        out_specs=[whole()] * parts,
        scratch_shapes=[pltpu.VMEM((height, width), jnp.bfloat16)],
        compiler_params=pltpu.CompilerParams(vmem_limit_bytes=GRANT),
        name="send_rows",
    )(*near(stats, arrived, basis, science, good, place))

    if not direct:
        result = lax.all_to_all(blocks[0], "det", split_axis=0, concat_axis=0, tiled=True)
        return result[None, None]
    arrivals = [blocks[0]]
    for d in range(1, owners):
        arrivals.append(
            lax.ppermute(blocks[d], "det", [(i, (i + d) % owners) for i in range(owners)])
        )
    result = None
    early = max(1, owners - 2)
    for shifts in (list(range(early)), list(range(early, owners))):
        former = [] if result is None else [result]
        result = pl.pallas_call(
            lambda *refs: collect_kernel(*refs, shifts=shifts),
            out_shape=pltpu.HBM((slots, width), jnp.bfloat16),
            in_specs=[whole()] * len(shifts) + [whole(pltpu.HBM)] * len(former),
            out_specs=whole(pltpu.HBM),
            scratch_shapes=[pltpu.SemaphoreType.DMA((len(shifts),))],
            input_output_aliases={len(shifts): 0} if former else {},
            compiler_params=pltpu.CompilerParams(vmem_limit_bytes=GRANT),
            name="collect",
        )(*near(*[arrivals[d] for d in shifts]), *far(*former))
    return result[None, None]


def solution(mesh):
    placed = (
        P(("det", "vis"), None),
        P("det", "vis", None, None),
        P("det", "vis", None, None),
        P("det", "vis", None),
        P("det", "vis", None, None),
    )
    return jax.shard_map(
        body, mesh=mesh, in_specs=placed, out_specs=P("det", "vis", None, None), check_vma=False
    )
```

```python
import jax
import jax.numpy as jnp
import numpy as np
from jax import lax
from jax.experimental import pallas as pl
from jax.experimental.pallas import tpu as pltpu
from jax.sharding import PartitionSpec as P


TAPS = 31
NB = 3
HALF = 15
HW = 23
DMAX = HW - HALF
EDGE = 32
LANES = 128
ROWS = 128
STATS = 16
DIRECT = 16
GUARD = 8
GRANT = 16 << 20

widths_list = (0.7, 1.5, 3.0)
epsilon = 1e-06


def tap_table():
    offsets = np.arange(TAPS, dtype=np.float32) - np.float32(HALF)
    widths = np.array(widths_list, dtype=np.float32)
    curves = np.exp(
        -(offsets[None, :] * offsets[None, :])
        / (np.float32(2.0) * widths[:, None] * widths[:, None])
    )
    curves = curves / np.sum(curves, axis=1, keepdims=True, dtype=np.float32)
    return curves.astype(jnp.dtype(jnp.bfloat16))


def band_at(curves, tap):
    inside = (tap >= 0) & (tap < TAPS)
    return np.where(inside, curves[:, np.clip(tap, 0, TAPS - 1)], 0).astype(curves.dtype)


def band_tables():
    curves = tap_table()
    span = 2 * DMAX
    inputs = np.arange(-GUARD, 2 * LANES + span)[:, None]
    across = band_at(curves, inputs - np.arange(LANES)[None, :] - span)
    across = np.transpose(across, (1, 0, 2)).reshape(-1, NB * LANES)
    outputs = np.arange(-GUARD, ROWS + span)[:, None]
    first = EDGE - HALF - DMAX
    downward = band_at(curves, np.arange(ROWS + 2 * EDGE)[None, :] - outputs - first)
    return jnp.asarray(across.astype(np.float32)), jnp.asarray(downward.astype(np.float32))


def arrange(area, own, other):
    parity = lax.axis_index("vis") % 2
    size = own.shape[0]

    @pl.when(parity == 0)
    def _():
        area[0:size, :] = own[...]
        area[size:, :] = other[...]

    @pl.when(parity == 1)
    def _():
        area[0:size, :] = other[...]
        area[size:, :] = own[...]


def smear(area, band, smeared):
    for at in range(0, smeared.shape[2], LANES):
        block = jnp.dot(
            area[:, at : at + 2 * LANES], band[...], preferred_element_type=jnp.float32
        ).astype(smeared.dtype)
        for b in range(NB):
            smeared[b, :, at : at + LANES] = block[:, b * LANES : (b + 1) * LANES]


def gather_sums(basis, science, good, offset, first, rows, sums):
    group = 16
    width = science.shape[1]

    def step(index, sums):
        here = pl.ds(pl.multiple_of(index * group + offset, group), group)
        there = pl.ds(pl.multiple_of(index * group + first, group), group)
        sums = list(sums)
        for at in range(0, width, LANES):
            cols = slice(at, at + LANES)
            weight = good[there, cols].astype(jnp.float32)
            signal = science[there, cols].astype(jnp.float32)
            terms = [weight * basis[b, here, cols] for b in range(NB)]
            lit = weight * signal
            values = [terms[k] * terms[l] for k in range(NB) for l in range(k, NB)]
            values += terms + [weight]
            values += [terms[k] * signal for k in range(NB)] + [lit, lit * signal]
            sums = [total + value for total, value in zip(sums, values)]
        return tuple(sums)

    if sums is None:
        sums = (jnp.zeros((group, LANES), jnp.float32),) * 15
    return lax.fori_loop(0, rows // group, step, sums)


def store_sums(stats, sums):
    for k, total in enumerate(sums):
        stats[k : k + 1, :] = jnp.sum(total, axis=0, keepdims=True)
    stats[15:16, :] = jnp.zeros((1, LANES), jnp.float32)


def inner_basis_kernel(own, other, band, column, smeared, basis, area):
    arrange(area, own, other)
    smear(area, band, smeared)
    rows = basis.shape[1]
    for at in range(0, rows, ROWS):
        size = min(ROWS, rows - at)
        reach = size + 2 * EDGE
        for b in range(NB):
            basis[b, at : at + size, :] = jnp.dot(
                column[b, 0:size, 0:reach], smeared[b, at : at + reach, :],
                preferred_element_type=jnp.float32,
            )


def inner_sums_kernel(basis, science, good, stats):
    store_sums(stats, gather_sums(basis, science, good, 0, EDGE, basis.shape[1], None))


def outer_kernel(
    own_edge, other_edge, inner, inner_stats, band, column, science, good, basis, stats, area, smeared
):
    arrange(area, own_edge, other_edge)
    smear(area, band, smeared)
    height = science.shape[0]
    for b in range(NB):
        near_rows = jnp.concatenate([smeared[b, 0:EDGE, :], inner[b, 0 : 2 * EDGE, :]], axis=0)
        far_rows = jnp.concatenate(
            [inner[b, height - 2 * EDGE :, :], smeared[b, EDGE : 2 * EDGE, :]], axis=0
        )
        taps = column[b, 0:EDGE, 0 : 3 * EDGE]
        basis[b, 0:EDGE, :] = jnp.dot(taps, near_rows, preferred_element_type=jnp.float32)
        basis[b, EDGE:, :] = jnp.dot(taps, far_rows, preferred_element_type=jnp.float32)
    sums = gather_sums(basis, science, good, 0, 0, EDGE, None)
    sums = gather_sums(basis, science, good, EDGE, height - EDGE, EDGE, sums)
    store_sums(stats, sums)
    stats[...] = stats[...] + inner_stats[...]


def edge_kernel(turned, own, edge, landing, sem):
    used = turned.shape[0]
    tail = used // LANES * LANES
    landing[tail:, :] = jnp.zeros((landing.shape[0] - tail, LANES), landing.dtype)
    copy = pltpu.make_async_copy(turned, landing.at[0:used, :], sem)
    copy.start()
    copy.wait()
    for at in range(0, landing.shape[0], LANES):
        own[:, at : at + LANES] = jnp.transpose(landing[at : at + LANES, :])
    start = lax.axis_index("vis") % 2 * (own.shape[0] - EDGE)
    edge[...] = own[pl.ds(pl.multiple_of(start, EDGE), EDGE), :]


def collect_kernel(*refs, shifts):
    blocks, result, sem = refs[: len(shifts)], refs[-2], refs[-1]
    at = lax.axis_index("det")
    owners = lax.axis_size("det")
    length = blocks[0].shape[0]
    copies = []
    for k, shift in enumerate(shifts):
        start = pl.multiple_of((at - shift + owners) % owners * length, length)
        copies.append(
            pltpu.make_async_copy(blocks[k], result.at[pl.ds(start, length), :], sem.at[k])
        )
    for copy in copies:
        copy.start()
    for copy in copies:
        copy.wait()


def prepare_kernel(
    dither, routes, across, downward, science, good,
    band, column, place, signal, weight, far_across, far_downward, shifts, targets, sem,
    *, owners, capacity, direct
):
    moves = (
        (routes, targets), (dither, shifts), (across, far_across), (downward, far_downward),
        (science, signal), (good, weight),
    )
    copies = [pltpu.make_async_copy(*move, sem.at[k]) for k, move in enumerate(moves)]
    for copy in copies:
        copy.start()
    copies[0].wait()
    rows = targets.shape[1]
    wanted = targets[...]
    if direct:
        wanted = wanted - lax.axis_index("det")
        wanted = jnp.where(wanted < 0, wanted + owners, wanted)
    chosen = lax.broadcasted_iota(jnp.int32, (owners, rows), 0) == wanted
    earlier = lax.broadcasted_iota(jnp.int32, (rows, rows), 0) < lax.broadcasted_iota(
        jnp.int32, (rows, rows), 1
    )
    before = jnp.dot(
        chosen.astype(jnp.float32).astype(jnp.bfloat16),
        earlier.astype(jnp.float32).astype(jnp.bfloat16),
        preferred_element_type=jnp.float32,
    )
    rank = jnp.sum(jnp.where(chosen, before, 0.0), axis=0, keepdims=True).astype(jnp.int32)
    slot = wanted * capacity + rank
    matches = lax.broadcasted_iota(jnp.int32, place.shape, 0) == slot
    place[...] = matches.astype(jnp.float32).astype(jnp.bfloat16)
    for copy in copies[1:4]:
        copy.wait()
    size = far_across.shape[0]
    turned = pltpu.roll(far_across[...], size - GUARD - DMAX + shifts[1], 0)
    band[...] = turned[: band.shape[0]].astype(band.dtype)
    size = far_downward.shape[1]
    for b in range(NB):
        turned = pltpu.roll(far_downward[b], size - GUARD - DMAX - shifts[0], 0)
        column[b] = turned[:ROWS].astype(column.dtype)
    for copy in copies[4:]:
        copy.wait()


def solve_small(gram, vector):
    size = NB + 1
    matrix = [[gram[r][c] + (1.0 if r == c else 0.0) for c in range(size)] for r in range(size)]
    lower = [[None] * size for _ in range(size)]
    for c in range(size):
        running = matrix[c][c]
        for k in range(c):
            running = running - lower[c][k] * lower[c][k]
        lower[c][c] = jnp.sqrt(running)
        for r in range(c + 1, size):
            running = matrix[r][c]
            for k in range(c):
                running = running - lower[r][k] * lower[c][k]
            lower[r][c] = running / lower[c][c]
    forward = []
    for r in range(size):
        running = vector[r]
        for c in range(r):
            running = running - lower[r][c] * forward[c]
        forward.append(running / lower[r][r])
    backward = [None] * size
    for r in range(size - 1, -1, -1):
        running = forward[r]
        for c in range(r + 1, size):
            running = running - lower[c][r] * backward[c]
        backward[r] = running / lower[r][r]
    return backward


def first_send_kernel(
    stats, arrived, inner, outer, science, good, place, out, significance, *, part
):
    totals = jnp.sum(stats[...] + arrived[...], axis=1, keepdims=True)
    value = [totals[k : k + 1, :] for k in range(15)]
    gram = [[None] * (NB + 1) for _ in range(NB + 1)]
    at = 0
    for k in range(NB):
        for l in range(k, NB):
            gram[k][l] = gram[l][k] = value[at]
            at += 1
    for k in range(NB + 1):
        gram[k][NB] = gram[NB][k] = value[at]
        at += 1
    moment = value[at : at + NB + 1]
    power = value[at + NB + 1]
    coeffs = solve_small(gram, moment)
    cross = sum(coeffs[k] * moment[k] for k in range(NB + 1))
    quadratic = sum(
        coeffs[k] * gram[k][l] * coeffs[l] for k in range(NB + 1) for l in range(NB + 1)
    )
    residual = power - 2.0 * cross + quadratic
    scale = 1.0 / jnp.sqrt(residual / (gram[NB][NB] + 1.0) + epsilon)

    height, width = science.shape
    group = 16
    spread = lambda x: jnp.broadcast_to(x, (group, LANES))
    weights = [spread(c) for c in coeffs]
    scale = spread(scale)

    def fill(basis, offset, first, rows):
        def step(index, carry):
            here = pl.ds(pl.multiple_of(index * group + offset, group), group)
            there = pl.ds(pl.multiple_of(index * group + first, group), group)
            for start in range(0, width, LANES):
                cols = slice(start, start + LANES)
                model = weights[0] * basis[0, here, cols]
                for b in range(1, NB):
                    model = model + weights[b] * basis[b, here, cols]
                model = model + weights[NB]
                difference = good[there, cols].astype(jnp.float32) * (
                    science[there, cols].astype(jnp.float32) - model
                )
                significance[there, cols] = (difference * scale).astype(jnp.bfloat16)
            return carry

        lax.fori_loop(0, rows // group, step, 0)

    fill(inner, 0, EDGE, height - 2 * EDGE)
    fill(outer, 0, 0, EDGE)
    fill(outer, EDGE, height - EDGE, EDGE)
    pick_rows(place, significance, out, part)


def pick_rows(place, significance, out, part):
    length = out.shape[0]
    out[...] = jnp.dot(
        place[part * length : (part + 1) * length, :], significance[...],
        preferred_element_type=jnp.float32,
    ).astype(jnp.bfloat16)


def send_kernel(significance, place, *outs, parts):
    for out, part in zip(outs, parts):
        pick_rows(place, significance, out, part)


def whole(memory=pltpu.VMEM):
    return pl.BlockSpec(memory_space=memory)


def near(*arrays):
    return [pltpu.with_memory_space_constraint(array, pltpu.VMEM) for array in arrays]


def far(*arrays):
    return [pltpu.with_memory_space_constraint(array, pltpu.HBM) for array in arrays]


def body(template, science, good_pixels, dither, routes):
    det_count = lax.axis_size("det")
    vis_count = lax.axis_size("vis")
    count = det_count * vis_count
    share = template.shape[0]
    height, width = science.shape[2:]
    both = ("det", "vis")

    padded = width + LANES
    own, outgoing = pl.pallas_call(
        edge_kernel,
        out_shape=(
            pltpu.VMEM((share, padded), template.dtype),
            pltpu.VMEM((EDGE, padded), template.dtype),
        ),
        in_specs=[whole(pltpu.HBM)],
        out_specs=(whole(), whole()),
        scratch_shapes=[pltpu.VMEM((padded, share), template.dtype), pltpu.SemaphoreType.DMA],
        compiler_params=pltpu.CompilerParams(vmem_limit_bytes=GRANT),
        name="edge",
    )(*far(template.T))
    seam = [(i, i + 1) for i in range(1, count - 1, 2)]
    own_edge = lax.ppermute(outgoing, both, seam + [(j, i) for i, j in seam])
    pairs = [(i, i ^ 1) for i in range(vis_count)]
    other = lax.ppermute(own, "vis", pairs)

    owners = det_count
    capacity = max(2, 2 * height // owners)
    slots = owners * capacity
    direct = owners <= DIRECT
    targets = routes.reshape(1, height)
    tables = band_tables()
    band, column, place, science, good = pl.pallas_call(
        lambda *refs: prepare_kernel(*refs, owners=owners, capacity=capacity, direct=direct),
        out_shape=(
            pltpu.VMEM((2 * LANES, NB * LANES), jnp.bfloat16),
            pltpu.VMEM((NB, ROWS, ROWS + 2 * EDGE), jnp.bfloat16),
            pltpu.VMEM((slots, height), jnp.bfloat16),
            pltpu.VMEM((height, width), science.dtype),
            pltpu.VMEM((height, width), good_pixels.dtype),
        ),
        in_specs=[whole(pltpu.HBM)] * 6,
        out_specs=(whole(),) * 5,
        scratch_shapes=[pltpu.VMEM(table.shape, table.dtype) for table in tables]
        + [pltpu.SMEM((2,), jnp.int32), pltpu.VMEM((1, height), jnp.int32)]
        + [pltpu.SemaphoreType.DMA((6,))],
        compiler_params=pltpu.CompilerParams(vmem_limit_bytes=GRANT),
        name="prepare",
    )(*far(dither.reshape(2), targets, *tables, science[0, 0], good_pixels[0, 0]))
    params = pltpu.CompilerParams(vmem_limit_bytes=GRANT)
    inner_smeared, inner = pl.pallas_call(
        inner_basis_kernel,
        out_shape=(
            pltpu.VMEM((NB, 2 * share, width), jnp.bfloat16),
            pltpu.VMEM((NB, height - 2 * EDGE, width), jnp.float32),
        ),
        in_specs=[whole()] * 4,
        out_specs=(whole(), whole()),
        scratch_shapes=[pltpu.VMEM((2 * share, padded), jnp.bfloat16)],
        compiler_params=params,
        name="inner_basis",
    )(*near(own, other, band, column))
    other_edge = lax.ppermute(own_edge, "vis", pairs)
    inner_stats = pl.pallas_call(
        inner_sums_kernel,
        out_shape=pltpu.VMEM((STATS, LANES), jnp.float32),
        in_specs=[whole()] * 3,
        out_specs=whole(),
        compiler_params=params,
        name="inner_sums",
    )(*near(inner, science, good))
    outer, stats = pl.pallas_call(
        outer_kernel,
        out_shape=(
            pltpu.VMEM((NB, 2 * EDGE, width), jnp.float32),
            pltpu.VMEM((STATS, LANES), jnp.float32),
        ),
        in_specs=[whole()] * 8,
        out_specs=(whole(), whole()),
        scratch_shapes=[
            pltpu.VMEM((2 * EDGE, padded), jnp.bfloat16),
            pltpu.VMEM((NB, 2 * EDGE, width), jnp.bfloat16),
        ],
        compiler_params=params,
        name="outer",
    )(*near(own_edge, other_edge, inner_smeared, inner_stats, band, column, science, good))

    arrived = jnp.zeros_like(stats)
    for axis, size, first in (("det", det_count, 1), ("vis", vis_count, 2)):
        stride = first
        while stride < size:
            stats = stats + arrived
            arrived = lax.ppermute(stats, axis, [(i, i ^ stride) for i in range(size)])
            stride *= 2

    parts = owners if direct else 1
    length = slots // parts
    order = [4, 3, 5, 1, 7, 2, 6] if owners == 8 else list(range(1, parts))
    order = order + [0]
    first, significance = pl.pallas_call(
        lambda *refs: first_send_kernel(*refs, part=order[0]),
        out_shape=(
            pltpu.VMEM((length, width), jnp.bfloat16),
            pltpu.VMEM((height, width), jnp.bfloat16),
        ),
        in_specs=[whole()] * 7,
        out_specs=(whole(), whole()),
        compiler_params=params,
        name="first_rows",
    )(*near(stats, arrived, inner, outer, science, good, place))
    if not direct:
        result = lax.all_to_all(first, "det", split_axis=0, concat_axis=0, tiled=True)
        return result[None, None]
    blocks = pl.pallas_call(
        lambda *refs: send_kernel(*refs, parts=order[1:]),
        out_shape=[pltpu.VMEM((length, width), jnp.bfloat16)] * (parts - 1),
        in_specs=[whole()] * 2,
        out_specs=[whole()] * (parts - 1),
        compiler_params=params,
        name="send_rows",
    )(*near(significance, place))
    arrivals = dict(zip(order, [first] + list(blocks)))
    for d in order[:-1]:
        arrivals[d] = lax.ppermute(
            arrivals[d], "det", [(i, (i + d) % owners) for i in range(owners)]
        )
    result = None
    for shifts in ([0] + order[:-1],):
        former = [] if result is None else [result]
        result = pl.pallas_call(
            lambda *refs: collect_kernel(*refs, shifts=shifts),
            out_shape=pltpu.HBM((slots, width), jnp.bfloat16),
            in_specs=[whole()] * len(shifts) + [whole(pltpu.HBM)] * len(former),
            out_specs=whole(pltpu.HBM),
            scratch_shapes=[pltpu.SemaphoreType.DMA((len(shifts),))],
            input_output_aliases={len(shifts): 0} if former else {},
            compiler_params=pltpu.CompilerParams(vmem_limit_bytes=GRANT),
            name="collect",
        )(*near(*[arrivals[d] for d in shifts]), *far(*former))
    return result[None, None]


def solution(mesh):
    placed = (
        P(("det", "vis"), None),
        P("det", "vis", None, None),
        P("det", "vis", None, None),
        P("det", "vis", None),
        P("det", "vis", None, None),
    )
    return jax.shard_map(
        body, mesh=mesh, in_specs=placed, out_specs=P("det", "vis", None, None), check_vma=False
    )
```

```python
import jax
import jax.numpy as jnp
import numpy as np
from jax import lax
from jax.experimental import pallas as pl
from jax.experimental.pallas import tpu as pltpu
from jax.sharding import PartitionSpec as P


TAPS = 31
NB = 3
HALF = 15
HW = 23
DMAX = HW - HALF
EDGE = 32
LANES = 128
ROWS = 128
STATS = 16
DIRECT = 16
GUARD = 8
GRANT = 16 << 20

widths_list = (0.7, 1.5, 3.0)
epsilon = 1e-06


def tap_table():
    offsets = np.arange(TAPS, dtype=np.float32) - np.float32(HALF)
    widths = np.array(widths_list, dtype=np.float32)
    curves = np.exp(
        -(offsets[None, :] * offsets[None, :])
        / (np.float32(2.0) * widths[:, None] * widths[:, None])
    )
    curves = curves / np.sum(curves, axis=1, keepdims=True, dtype=np.float32)
    return curves.astype(jnp.dtype(jnp.bfloat16))


def band_at(curves, tap):
    inside = (tap >= 0) & (tap < TAPS)
    return np.where(inside, curves[:, np.clip(tap, 0, TAPS - 1)], 0).astype(curves.dtype)


def band_tables():
    curves = tap_table()
    span = 2 * DMAX
    inputs = np.arange(-GUARD, 2 * LANES + span)[:, None]
    across = band_at(curves, inputs - np.arange(LANES)[None, :] - span)
    across = np.transpose(across, (1, 0, 2)).reshape(-1, NB * LANES)
    outputs = np.arange(-GUARD, ROWS + span)[:, None]
    first = EDGE - HALF - DMAX
    downward = band_at(curves, np.arange(ROWS + 2 * EDGE)[None, :] - outputs - first)
    return jnp.asarray(across.astype(np.float32)), jnp.asarray(downward.astype(np.float32))


def arrange(area, own, other):
    parity = lax.axis_index("vis") % 2
    size = own.shape[0]

    @pl.when(parity == 0)
    def _():
        area[0:size, :] = own[...]
        area[size:, :] = other[...]

    @pl.when(parity == 1)
    def _():
        area[0:size, :] = other[...]
        area[size:, :] = own[...]


def smear(area, band, smeared):
    for at in range(0, smeared.shape[2], LANES):
        block = jnp.dot(
            area[:, at : at + 2 * LANES], band[...], preferred_element_type=jnp.float32
        ).astype(smeared.dtype)
        for b in range(NB):
            smeared[b, :, at : at + LANES] = block[:, b * LANES : (b + 1) * LANES]


def gather_sums(basis, science, good, offset, first, rows, sums):
    group = 16
    width = science.shape[1]

    def step(index, sums):
        here = pl.ds(pl.multiple_of(index * group + offset, group), group)
        there = pl.ds(pl.multiple_of(index * group + first, group), group)
        sums = list(sums)
        for at in range(0, width, LANES):
            cols = slice(at, at + LANES)
            weight = good[there, cols].astype(jnp.float32)
            signal = science[there, cols].astype(jnp.float32)
            terms = [weight * basis[b, here, cols] for b in range(NB)]
            lit = weight * signal
            values = [terms[k] * terms[l] for k in range(NB) for l in range(k, NB)]
            values += terms + [weight]
            values += [terms[k] * signal for k in range(NB)] + [lit, lit * signal]
            sums = [total + value for total, value in zip(sums, values)]
        return tuple(sums)

    if sums is None:
        sums = (jnp.zeros((group, LANES), jnp.float32),) * 15
    return lax.fori_loop(0, rows // group, step, sums)


def store_sums(stats, sums):
    for k, total in enumerate(sums):
        stats[k : k + 1, :] = jnp.sum(total, axis=0, keepdims=True)
    stats[15:16, :] = jnp.zeros((1, LANES), jnp.float32)


def inner_basis_kernel(own, other, band, column, smeared, basis, area):
    arrange(area, own, other)
    smear(area, band, smeared)
    rows = basis.shape[1]
    for at in range(0, rows, ROWS):
        size = min(ROWS, rows - at)
        reach = size + 2 * EDGE
        for b in range(NB):
            basis[b, at : at + size, :] = jnp.dot(
                column[b, 0:size, 0:reach], smeared[b, at : at + reach, :],
                preferred_element_type=jnp.float32,
            )


def inner_sums_kernel(basis, science, good, stats):
    store_sums(stats, gather_sums(basis, science, good, 0, EDGE, basis.shape[1], None))


def outer_kernel(
    own_edge, other_edge, inner, inner_stats, band, column, science, good, basis, stats, area, smeared
):
    arrange(area, own_edge, other_edge)
    smear(area, band, smeared)
    height = science.shape[0]
    for b in range(NB):
        near_rows = jnp.concatenate([smeared[b, 0:EDGE, :], inner[b, 0 : 2 * EDGE, :]], axis=0)
        far_rows = jnp.concatenate(
            [inner[b, height - 2 * EDGE :, :], smeared[b, EDGE : 2 * EDGE, :]], axis=0
        )
        taps = column[b, 0:EDGE, 0 : 3 * EDGE]
        basis[b, 0:EDGE, :] = jnp.dot(taps, near_rows, preferred_element_type=jnp.float32)
        basis[b, EDGE:, :] = jnp.dot(taps, far_rows, preferred_element_type=jnp.float32)
    sums = gather_sums(basis, science, good, 0, 0, EDGE, None)
    sums = gather_sums(basis, science, good, EDGE, height - EDGE, EDGE, sums)
    store_sums(stats, sums)
    stats[...] = stats[...] + inner_stats[...]


def edge_kernel(turned, own, edge, landing, sem):
    used = turned.shape[0]
    tail = used // LANES * LANES
    landing[tail:, :] = jnp.zeros((landing.shape[0] - tail, LANES), landing.dtype)
    copy = pltpu.make_async_copy(turned, landing.at[0:used, :], sem)
    copy.start()
    copy.wait()
    for at in range(0, landing.shape[0], LANES):
        own[:, at : at + LANES] = jnp.transpose(landing[at : at + LANES, :])
    start = lax.axis_index("vis") % 2 * (own.shape[0] - EDGE)
    edge[...] = own[pl.ds(pl.multiple_of(start, EDGE), EDGE), :]


def collect_kernel(*refs, shifts):
    blocks, result, sem = refs[: len(shifts)], refs[-2], refs[-1]
    at = lax.axis_index("det")
    owners = lax.axis_size("det")
    length = blocks[0].shape[0]
    copies = []
    for k, shift in enumerate(shifts):
        start = pl.multiple_of((at - shift + owners) % owners * length, length)
        copies.append(
            pltpu.make_async_copy(blocks[k], result.at[pl.ds(start, length), :], sem.at[k])
        )
    for copy in copies:
        copy.start()
    for copy in copies:
        copy.wait()


def prepare_kernel(
    dither, routes, across, downward, science, good,
    band, column, place, signal, weight, far_across, far_downward, shifts, targets, sem,
    *, owners, capacity, direct
):
    moves = (
        (routes, targets), (dither, shifts), (across, far_across), (downward, far_downward),
        (science, signal), (good, weight),
    )
    copies = [pltpu.make_async_copy(*move, sem.at[k]) for k, move in enumerate(moves)]
    for copy in copies:
        copy.start()
    copies[0].wait()
    rows = targets.shape[1]
    wanted = targets[...]
    if direct:
        wanted = wanted - lax.axis_index("det")
        wanted = jnp.where(wanted < 0, wanted + owners, wanted)
    chosen = lax.broadcasted_iota(jnp.int32, (owners, rows), 0) == wanted
    earlier = lax.broadcasted_iota(jnp.int32, (rows, rows), 0) < lax.broadcasted_iota(
        jnp.int32, (rows, rows), 1
    )
    before = jnp.dot(
        chosen.astype(jnp.float32).astype(jnp.bfloat16),
        earlier.astype(jnp.float32).astype(jnp.bfloat16),
        preferred_element_type=jnp.float32,
    )
    rank = jnp.sum(jnp.where(chosen, before, 0.0), axis=0, keepdims=True).astype(jnp.int32)
    slot = wanted * capacity + rank
    matches = lax.broadcasted_iota(jnp.int32, place.shape, 0) == slot
    place[...] = matches.astype(jnp.float32).astype(jnp.bfloat16)
    for copy in copies[1:4]:
        copy.wait()
    size = far_across.shape[0]
    turned = pltpu.roll(far_across[...], size - GUARD - DMAX + shifts[1], 0)
    band[...] = turned[: band.shape[0]].astype(band.dtype)
    size = far_downward.shape[1]
    for b in range(NB):
        turned = pltpu.roll(far_downward[b], size - GUARD - DMAX - shifts[0], 0)
        column[b] = turned[:ROWS].astype(column.dtype)
    for copy in copies[4:]:
        copy.wait()


def solve_small(gram, vector):
    size = NB + 1
    matrix = [[gram[r][c] + (1.0 if r == c else 0.0) for c in range(size)] for r in range(size)]
    lower = [[None] * size for _ in range(size)]
    for c in range(size):
        running = matrix[c][c]
        for k in range(c):
            running = running - lower[c][k] * lower[c][k]
        lower[c][c] = jnp.sqrt(running)
        for r in range(c + 1, size):
            running = matrix[r][c]
            for k in range(c):
                running = running - lower[r][k] * lower[c][k]
            lower[r][c] = running / lower[c][c]
    forward = []
    for r in range(size):
        running = vector[r]
        for c in range(r):
            running = running - lower[r][c] * forward[c]
        forward.append(running / lower[r][r])
    backward = [None] * size
    for r in range(size - 1, -1, -1):
        running = forward[r]
        for c in range(r + 1, size):
            running = running - lower[c][r] * backward[c]
        backward[r] = running / lower[r][r]
    return backward


def first_send_kernel(stats, *refs, part):
    arrived, refs = refs[:-7], refs[-7:]
    inner, outer, science, good, place, out, significance = refs
    totals = jnp.sum(
        sum([array[...] for array in arrived], start=stats[...]), axis=1, keepdims=True
    )
    value = [totals[k : k + 1, :] for k in range(15)]
    gram = [[None] * (NB + 1) for _ in range(NB + 1)]
    at = 0
    for k in range(NB):
        for l in range(k, NB):
            gram[k][l] = gram[l][k] = value[at]
            at += 1
    for k in range(NB + 1):
        gram[k][NB] = gram[NB][k] = value[at]
        at += 1
    moment = value[at : at + NB + 1]
    power = value[at + NB + 1]
    coeffs = solve_small(gram, moment)
    cross = sum(coeffs[k] * moment[k] for k in range(NB + 1))
    quadratic = sum(
        coeffs[k] * gram[k][l] * coeffs[l] for k in range(NB + 1) for l in range(NB + 1)
    )
    residual = power - 2.0 * cross + quadratic
    scale = 1.0 / jnp.sqrt(residual / (gram[NB][NB] + 1.0) + epsilon)

    height, width = science.shape
    group = 16
    spread = lambda x: jnp.broadcast_to(x, (group, LANES))
    weights = [spread(c) for c in coeffs]
    scale = spread(scale)

    def fill(basis, offset, first, rows):
        def step(index, carry):
            here = pl.ds(pl.multiple_of(index * group + offset, group), group)
            there = pl.ds(pl.multiple_of(index * group + first, group), group)
            for start in range(0, width, LANES):
                cols = slice(start, start + LANES)
                model = weights[0] * basis[0, here, cols]
                for b in range(1, NB):
                    model = model + weights[b] * basis[b, here, cols]
                model = model + weights[NB]
                difference = good[there, cols].astype(jnp.float32) * (
                    science[there, cols].astype(jnp.float32) - model
                )
                significance[there, cols] = (difference * scale).astype(jnp.bfloat16)
            return carry

        lax.fori_loop(0, rows // group, step, 0)

    fill(inner, 0, EDGE, height - 2 * EDGE)
    fill(outer, 0, 0, EDGE)
    fill(outer, EDGE, height - EDGE, EDGE)
    pick_rows(place, significance, out, part)


def pick_rows(place, significance, out, part):
    length = out.shape[0]
    out[...] = jnp.dot(
        place[part * length : (part + 1) * length, :], significance[...],
        preferred_element_type=jnp.float32,
    ).astype(jnp.bfloat16)


def send_kernel(significance, place, *outs, parts):
    for out, part in zip(outs, parts):
        pick_rows(place, significance, out, part)


def whole(memory=pltpu.VMEM):
    return pl.BlockSpec(memory_space=memory)


def near(*arrays):
    return [pltpu.with_memory_space_constraint(array, pltpu.VMEM) for array in arrays]


def far(*arrays):
    return [pltpu.with_memory_space_constraint(array, pltpu.HBM) for array in arrays]


def body(template, science, good_pixels, dither, routes):
    det_count = lax.axis_size("det")
    vis_count = lax.axis_size("vis")
    count = det_count * vis_count
    share = template.shape[0]
    height, width = science.shape[2:]
    both = ("det", "vis")

    padded = width + LANES
    own, outgoing = pl.pallas_call(
        edge_kernel,
        out_shape=(
            pltpu.VMEM((share, padded), template.dtype),
            pltpu.VMEM((EDGE, padded), template.dtype),
        ),
        in_specs=[whole(pltpu.HBM)],
        out_specs=(whole(), whole()),
        scratch_shapes=[pltpu.VMEM((padded, share), template.dtype), pltpu.SemaphoreType.DMA],
        compiler_params=pltpu.CompilerParams(vmem_limit_bytes=GRANT),
        name="edge",
    )(*far(template.T))
    seam = [(i, i + 1) for i in range(1, count - 1, 2)]
    own_edge = lax.ppermute(outgoing, both, seam + [(j, i) for i, j in seam])
    pairs = [(i, i ^ 1) for i in range(vis_count)]
    other = lax.ppermute(own, "vis", pairs)

    owners = det_count
    capacity = max(2, 2 * height // owners)
    slots = owners * capacity
    direct = owners <= DIRECT
    targets = routes.reshape(1, height)
    tables = band_tables()
    band, column, place, science, good = pl.pallas_call(
        lambda *refs: prepare_kernel(*refs, owners=owners, capacity=capacity, direct=direct),
        out_shape=(
            pltpu.VMEM((2 * LANES, NB * LANES), jnp.bfloat16),
            pltpu.VMEM((NB, ROWS, ROWS + 2 * EDGE), jnp.bfloat16),
            pltpu.VMEM((slots, height), jnp.bfloat16),
            pltpu.VMEM((height, width), science.dtype),
            pltpu.VMEM((height, width), good_pixels.dtype),
        ),
        in_specs=[whole(pltpu.HBM)] * 6,
        out_specs=(whole(),) * 5,
        scratch_shapes=[pltpu.VMEM(table.shape, table.dtype) for table in tables]
        + [pltpu.SMEM((2,), jnp.int32), pltpu.VMEM((1, height), jnp.int32)]
        + [pltpu.SemaphoreType.DMA((6,))],
        compiler_params=pltpu.CompilerParams(vmem_limit_bytes=GRANT),
        name="prepare",
    )(*far(dither.reshape(2), targets, *tables, science[0, 0], good_pixels[0, 0]))
    params = pltpu.CompilerParams(vmem_limit_bytes=GRANT)
    inner_smeared, inner = pl.pallas_call(
        inner_basis_kernel,
        out_shape=(
            pltpu.VMEM((NB, 2 * share, width), jnp.bfloat16),
            pltpu.VMEM((NB, height - 2 * EDGE, width), jnp.float32),
        ),
        in_specs=[whole()] * 4,
        out_specs=(whole(), whole()),
        scratch_shapes=[pltpu.VMEM((2 * share, padded), jnp.bfloat16)],
        compiler_params=params,
        name="inner_basis",
    )(*near(own, other, band, column))
    other_edge = lax.ppermute(own_edge, "vis", pairs)
    inner_stats = pl.pallas_call(
        inner_sums_kernel,
        out_shape=pltpu.VMEM((STATS, LANES), jnp.float32),
        in_specs=[whole()] * 3,
        out_specs=whole(),
        compiler_params=params,
        name="inner_sums",
    )(*near(inner, science, good))
    outer, stats = pl.pallas_call(
        outer_kernel,
        out_shape=(
            pltpu.VMEM((NB, 2 * EDGE, width), jnp.float32),
            pltpu.VMEM((STATS, LANES), jnp.float32),
        ),
        in_specs=[whole()] * 8,
        out_specs=(whole(), whole()),
        scratch_shapes=[
            pltpu.VMEM((2 * EDGE, padded), jnp.bfloat16),
            pltpu.VMEM((NB, 2 * EDGE, width), jnp.bfloat16),
        ],
        compiler_params=params,
        name="outer",
    )(*near(own_edge, other_edge, inner_smeared, inner_stats, band, column, science, good))

    if owners == 8 and vis_count == 4:
        waves = [(2, 4, 6), (8, 16, 24)]
    else:
        waves = [(vis_count << at,) for at in range(det_count.bit_length() - 1)] + [(2,)]
    for wave in waves[:-1]:
        stats = sum(
            [lax.ppermute(stats, both, [(i, i ^ bit) for i in range(count)]) for bit in wave],
            start=stats,
        )
    arrived = [
        lax.ppermute(stats, both, [(i, i ^ bit) for i in range(count)]) for bit in waves[-1]
    ]

    parts = owners if direct else 1
    length = slots // parts
    order = [4, 3, 5, 2, 6, 1, 7] if owners == 8 else list(range(1, parts))
    order = order + [0]
    first, significance = pl.pallas_call(
        lambda *refs: first_send_kernel(*refs, part=order[0]),
        out_shape=(
            pltpu.VMEM((length, width), jnp.bfloat16),
            pltpu.VMEM((height, width), jnp.bfloat16),
        ),
        in_specs=[whole()] * (6 + len(arrived)),
        out_specs=(whole(), whole()),
        compiler_params=params,
        name="first_rows",
    )(*near(stats, *arrived, inner, outer, science, good, place))
    if not direct:
        result = lax.all_to_all(first, "det", split_axis=0, concat_axis=0, tiled=True)
        return result[None, None]
    blocks = pl.pallas_call(
        lambda *refs: send_kernel(*refs, parts=order[1:]),
        out_shape=[pltpu.VMEM((length, width), jnp.bfloat16)] * (parts - 1),
        in_specs=[whole()] * 2,
        out_specs=[whole()] * (parts - 1),
        compiler_params=params,
        name="send_rows",
    )(*near(significance, place))
    arrivals = dict(zip(order, [first] + list(blocks)))
    for d in order[:-1]:
        arrivals[d] = lax.ppermute(
            arrivals[d], "det", [(i, (i + d) % owners) for i in range(owners)]
        )
    result = None
    for shifts in ([0] + order[:-3], order[-3:-1]):
        former = [] if result is None else [result]
        result = pl.pallas_call(
            lambda *refs: collect_kernel(*refs, shifts=shifts),
            out_shape=pltpu.HBM((slots, width), jnp.bfloat16),
            in_specs=[whole()] * len(shifts) + [whole(pltpu.HBM)] * len(former),
            out_specs=whole(pltpu.HBM),
            scratch_shapes=[pltpu.SemaphoreType.DMA((len(shifts),))],
            input_output_aliases={len(shifts): 0} if former else {},
            compiler_params=pltpu.CompilerParams(vmem_limit_bytes=GRANT),
            name="collect",
        )(*near(*[arrivals[d] for d in shifts]), *far(*former))
    return result[None, None]


def solution(mesh):
    placed = (
        P(("det", "vis"), None),
        P("det", "vis", None, None),
        P("det", "vis", None, None),
        P("det", "vis", None),
        P("det", "vis", None, None),
    )
    return jax.shard_map(
        body, mesh=mesh, in_specs=placed, out_specs=P("det", "vis", None, None), check_vma=False
    )
```
